512 devices in a mesh: ctx: 64 (over z, x_lo, core), head: 8 (over y, x_hi).
Axes of the slice: x: 4 (x_hi: 2, x_lo: 2; x = x_hi * 2 + x_lo), y: 4, z: 16, core: 2. Of those that a mesh axis runs over, the one named last changes fastest.
Arguments:
- queries: bfloat16 [65536, 4096], P(('ctx', 'head')), may hold values from -6 to 6
- keys: bfloat16 [65536, 1024], P(('ctx', 'head')), may hold values from -6 to 6
- values: bfloat16 [65536, 1024], P(('ctx', 'head')), may hold values from -1.5 to 1.5
- out_grad: bfloat16 [65536, 4096], P(('ctx', 'head')), may hold values from -6 to 6
- log_norm: float32 [65536, 32], P(('ctx', 'head')), may hold values from 2 to 4
- row_delta: float32 [65536, 32], P(('ctx', 'head')), may hold values from -10 to 10
- tile_pairs: int32 [64, 4, 16, 2], P('ctx'), may hold values from 0 to 7, as said below
- pair_count: int32 [64, 4], P('ctx'), may hold values from 0 to 16, as said below
Outputs:
- query_grad: bfloat16 [65536, 4096], P(('ctx', 'head'))
- key_grad: bfloat16 [65536, 1024], P(('ctx', 'head'))
- value_grad: bfloat16 [65536, 1024], P(('ctx', 'head'))
The draws below stay inside these ranges and needn't reach their ends.
Inputs may be any that keep to these rules, and one draw needn't show every extreme that they name: `tile_pairs`: Entries past pair_count are not read.
All inputs are finite; a program needn't handle non-finite values.
Results may differ from the reference program's by a relative error of at most 0.005.
Values may be sent and summed in bfloat16 or wider, within the bound.
A program may use at most 64 MiB of HBM per device.

```python
import jax
import jax.numpy as jnp
from jax import lax

HEAD_DIM = 128
Q_HEADS = 32
KV_HEADS = 8
TILE = 128
WIN = 4
BLOCK = 1024
TPB = 8
LIST_SLOTS = 16
SEQ = 65536
N_CTX = 64


def list_structure(key):
    all_pairs = TPB * TPB
    pair_index = jnp.arange(all_pairs, dtype=jnp.int32)
    query_part = pair_index // TPB
    key_part = pair_index % TPB
    lower_total = TPB * (TPB - 1) // 2
    extra_most = min(TPB, lower_total)
    base_key = jax.random.fold_in(key, 17)

    def one_list(block, cycle_step):
        list_key = jax.random.fold_in(base_key, block * WIN + cycle_step)
        key_perm, key_count, key_extra = jax.random.split(list_key, 3)
        ranks = jax.random.permutation(key_perm, all_pairs).astype(jnp.int32)
        level = jnp.where(query_part == key_part, 0, jnp.where(key_part < query_part, 1, 2)).astype(jnp.int32)
        first_key = level * all_pairs + ranks
        sort_key = jnp.where(cycle_step == 0, first_key, ranks)
        ordering = jnp.argsort(sort_key)[:LIST_SLOTS].astype(jnp.int32)
        later_count = jax.random.randint(key_count, (), 0, LIST_SLOTS + 1)
        later_count = jnp.where((block == WIN) & (cycle_step == 1), LIST_SLOTS, later_count)
        later_count = jnp.where(block == cycle_step, LIST_SLOTS, later_count)
        later_count = jnp.where(block < cycle_step, 0, later_count)
        first_count = TPB + jax.random.randint(key_extra, (), 0, extra_most + 1)
        count = jnp.where(cycle_step == 0, first_count, later_count).astype(jnp.int32)
        pairs = jnp.stack([ordering // TPB, ordering % TPB], axis=-1).astype(jnp.int32)
        return (pairs, count)
    blocks = jnp.arange(N_CTX, dtype=jnp.int32)
    cycle_steps = jnp.arange(WIN, dtype=jnp.int32)
    per_step = jax.vmap(one_list, in_axes=(None, 0))
    return jax.vmap(per_step, in_axes=(0, None))(blocks, cycle_steps)


def draw_tile_pairs(key, part):
    return list_structure(key)[0]


def draw_pair_count(key, part):
    return list_structure(key)[1]


def block_scale(key, dims, shards, least, high):
    factor_of = 1.0
    for axis_at, blocks in shards:
        draws = jax.random.uniform(jax.random.fold_in(jax.random.fold_in(key, 6), axis_at), (blocks,), jnp.float32, least / len(shards), high / len(shards))
        factor_of = factor_of * jnp.repeat(jnp.exp(draws), dims[axis_at] // blocks).reshape((-1,) + (1,) * (len(dims) - 1 - axis_at))
    return factor_of


def scatter_about(rng, shape, width, bound, cuts=(), kind=jnp.bfloat16):
    entries = jax.random.normal(rng, shape, jnp.float32) * width
    if len(cuts) > 0:
        entries = block_scale(rng, shape, cuts, -0.22, 0.18) * entries
    return jnp.clip(entries, min=-bound, max=bound).astype(kind)


def setup_inputs(seed: int = 0) -> dict:
    seeds = jax.random.split(jax.random.key(seed), 9)
    return {
        "queries": scatter_about(seeds[0], (SEQ, Q_HEADS * HEAD_DIM), 1.0, 6.0, ((0, 512),)),
        "keys": scatter_about(seeds[1], (SEQ, KV_HEADS * HEAD_DIM), 1.0, 6.0, ((0, 512),)),
        "values": scatter_about(seeds[2], (SEQ, KV_HEADS * HEAD_DIM), 0.25, 1.5, ((0, 512),)),
        "out_grad": scatter_about(seeds[3], (SEQ, Q_HEADS * HEAD_DIM), 1.0, 6.0, ((0, 512),)),
        "log_norm": jnp.clip(2.0 + 2.0 * jax.random.uniform(seeds[4], (SEQ, Q_HEADS), jnp.float32) ** block_scale(seeds[4], (SEQ, Q_HEADS), ((0, 512),), -0.2, 0.2), 2.0, 4.0),
        "row_delta": scatter_about(seeds[5], (SEQ, Q_HEADS), 2.0, 10.0, ((0, 512),), jnp.float32),
        "tile_pairs": draw_tile_pairs(jax.random.fold_in(seeds[8], 71), 0),
        "pair_count": draw_pair_count(jax.random.fold_in(seeds[8], 71), 0),
    }


def tile_terms(query_tile, grad_tile, norm_tile, delta_tile, key_tile, value_tile, allowed, scaling):
    scores = jnp.einsum("ikgd,jkd->kgij", query_tile, key_tile) * scaling
    probs = jnp.where(allowed, jnp.exp(scores - norm_tile), 0.0)
    prob_grad = jnp.einsum("ikgd,jkd->kgij", grad_tile, value_tile)
    score_low = (scaling * probs * (prob_grad - delta_tile)).astype(jnp.bfloat16)
    score_grad = lax.optimization_barrier(score_low).astype(jnp.float32)
    probs_low = lax.optimization_barrier(probs.astype(jnp.bfloat16)).astype(jnp.float32)
    query_term = jnp.einsum("kgij,jkd->ikgd", score_grad, key_tile)
    key_term = jnp.einsum("kgij,ikgd->jkd", score_grad, query_tile)
    value_term = jnp.einsum("kgij,ikgd->jkd", probs_low, grad_tile)
    return query_term, key_term, value_term


def add_rows(total, term, start):
    current = lax.dynamic_slice_in_dim(total, start, term.shape[0], 0)
    return lax.dynamic_update_slice_in_dim(total, current + term, start, 0)


def reference(queries, keys, values, out_grad, log_norm, row_delta, tile_pairs, pair_count):
    scaling = HEAD_DIM ** -0.5
    group_size = Q_HEADS // KV_HEADS
    query_blocks = queries.reshape(N_CTX, BLOCK, KV_HEADS, group_size, HEAD_DIM)
    grad_blocks = out_grad.reshape(N_CTX, BLOCK, KV_HEADS, group_size, HEAD_DIM)
    key_blocks = keys.reshape(N_CTX, BLOCK, KV_HEADS, HEAD_DIM)
    value_blocks = values.reshape(N_CTX, BLOCK, KV_HEADS, HEAD_DIM)
    norm_blocks = log_norm.reshape(N_CTX, BLOCK, KV_HEADS, group_size)
    delta_blocks = row_delta.reshape(N_CTX, BLOCK, KV_HEADS, group_size)
    positions = jnp.arange(TILE, dtype=jnp.int32)
    lower_tri = positions[None, :] <= positions[:, None]

    def one_block(carry, index):
        key_total, value_total = carry
        query_rows = query_blocks[index].astype(jnp.float32)
        grad_rows = grad_blocks[index].astype(jnp.float32)
        norm_cols = jnp.transpose(norm_blocks[index], (1, 2, 0))[..., None]
        delta_cols = jnp.transpose(delta_blocks[index], (1, 2, 0))[..., None]
        query_total = jnp.zeros((BLOCK, KV_HEADS, group_size, HEAD_DIM), jnp.float32)
        for cycle_step in range(WIN):
            source = ((index - cycle_step) % N_CTX).astype(jnp.int32)
            key_rows = key_blocks[source].astype(jnp.float32)
            value_rows = value_blocks[source].astype(jnp.float32)
            pair_list = tile_pairs[index, cycle_step]
            live_count = pair_count[index, cycle_step]
            causal = cycle_step == 0

            def slot_body(slot, state):
                q_total, k_total, v_total = state
                q_start = (pair_list[slot, 0] * TILE).astype(jnp.int32)
                k_start = (pair_list[slot, 1] * TILE).astype(jnp.int32)
                if causal:
                    allowed = (q_start != k_start) | lower_tri
                else:
                    allowed = jnp.ones((TILE, TILE), bool)
                query_term, key_term, value_term = tile_terms(
                    lax.dynamic_slice_in_dim(query_rows, q_start, TILE, 0),
                    lax.dynamic_slice_in_dim(grad_rows, q_start, TILE, 0),
                    lax.dynamic_slice_in_dim(norm_cols, q_start, TILE, 2),
                    lax.dynamic_slice_in_dim(delta_cols, q_start, TILE, 2),
                    lax.dynamic_slice_in_dim(key_rows, k_start, TILE, 0),
                    lax.dynamic_slice_in_dim(value_rows, k_start, TILE, 0),
                    allowed, scaling)
                global_row = (source * BLOCK + k_start).astype(jnp.int32)
                return (add_rows(q_total, query_term, q_start), add_rows(k_total, key_term, global_row), add_rows(v_total, value_term, global_row))

            query_total, key_total, value_total = lax.fori_loop(jnp.int32(0), live_count.astype(jnp.int32), slot_body, (query_total, key_total, value_total))
        return (key_total, value_total), query_total.reshape(BLOCK, Q_HEADS * HEAD_DIM).astype(jnp.bfloat16)

    start_total = jnp.zeros((SEQ, KV_HEADS, HEAD_DIM), jnp.float32)
    (key_total, value_total), query_parts = lax.scan(one_block, (start_total, start_total), jnp.arange(N_CTX, dtype=jnp.int32))
    query_grad = query_parts.reshape(SEQ, Q_HEADS * HEAD_DIM)
    key_grad = key_total.reshape(SEQ, KV_HEADS * HEAD_DIM).astype(jnp.bfloat16)
    value_grad = value_total.reshape(SEQ, KV_HEADS * HEAD_DIM).astype(jnp.bfloat16)
    return (query_grad, key_grad, value_grad)
```

```python
import functools

import jax
import jax.numpy as jnp
from jax import lax
from jax.experimental import pallas as pl
from jax.experimental.pallas import tpu as pltpu
from jax.sharding import PartitionSpec as P

HEAD_DIM = 128
TILE = 128
TPB = 8
WIN = 4
SLOTS = 16
GROUP = 4
WIDTH = GROUP * HEAD_DIM
SCALE = HEAD_DIM ** (-0.5)
LOG2E = 1.4426950408889634
MESH = pl.DeviceIdType.MESH


def wrap(value, size):
    return lax.rem(value + size, size)


def greet(ctx, head):
    n_ctx, n_head = lax.axis_size("ctx"), lax.axis_size("head")
    barrier = pltpu.get_barrier_semaphore()
    for d in range(1, n_head):
        pl.semaphore_signal(
            barrier, inc=1, device_id=(ctx, wrap(head + d, n_head)), device_id_type=MESH
        )
    for s in range(1, WIN):
        for there in (wrap(ctx + s, n_ctx), wrap(ctx - s, n_ctx)):
            pl.semaphore_signal(barrier, inc=1, device_id=(there, head), device_id_type=MESH)
    pl.semaphore_wait(barrier, n_head - 1 + 2 * (WIN - 1))


def gather_kernel(
    q_in, g_in, k_in, v_in, nd_in, q_out, g_out, k_out, v_out, nd_out,
    q_tmp, g_tmp, k_tmp, v_tmp, nd_tmp, send, recv, win_send, win_recv, own_in, own_out,
):
    ctx, head = lax.axis_index("ctx"), lax.axis_index("head")
    n_ctx, n_head = lax.axis_size("ctx"), lax.axis_size("head")

    def cut(which, j):
        if which == 0:
            return k_in.at[:, pl.ds(pl.multiple_of(j * HEAD_DIM, HEAD_DIM), HEAD_DIM)]
        if which == 1:
            return v_in.at[:, pl.ds(pl.multiple_of(j * HEAD_DIM, HEAD_DIM), HEAD_DIM)]
        if which == 2:
            return nd_in.at[j]
        if which == 3:
            return q_in.at[:, pl.ds(pl.multiple_of(j * WIDTH, WIDTH), WIDTH)]
        return g_in.at[:, pl.ds(pl.multiple_of(j * WIDTH, WIDTH), WIDTH)]

    def place(which, t):
        if which == 0:
            return k_out.at[0, t]
        if which == 1:
            return v_out.at[0, t]
        return (nd_out, q_out, g_out)[which - 2].at[t]

    temps = (k_tmp, v_tmp, nd_tmp, q_tmp, g_tmp)
    loads = [
        pltpu.make_async_copy(cut(w, head), temps[w], own_in.at[w]) for w in range(5)
    ]
    for load in loads:
        load.start()

    greet(ctx, head)

    def copy(which, d):
        j = wrap(head + d, n_head)
        return pltpu.make_async_remote_copy(
            src_ref=cut(which, j),
            dst_ref=place(which, head),
            send_sem=send.at[which, d],
            recv_sem=recv.at[which, d],
            device_id=(ctx, j),
            device_id_type=MESH,
        )

    copies = {(w, d): copy(w, d) for w in range(5) for d in range(1, n_head)}
    for w in (0, 1, 2, 3):
        for d in range(1, n_head):
            copies[w, d].start()
    stores = [
        pltpu.make_async_copy(temps[w], place(w, head), own_out.at[w]) for w in range(5)
    ]
    for w in range(5):
        loads[w].wait()
        stores[w].start()
    windows = []
    for which, out in ((0, k_out), (1, v_out)):
        stores[which].wait()
        for d in range(1, n_head):
            copies[which, d].wait_recv()
        for s in range(1, WIN):
            window = pltpu.make_async_remote_copy(
                src_ref=out.at[0],
                dst_ref=out.at[s],
                send_sem=win_send.at[which, s],
                recv_sem=win_recv.at[which, s],
                device_id=(wrap(ctx + s, n_ctx), head),
                device_id_type=MESH,
            )
            window.start()
            windows.append(window)
    for d in range(1, n_head):
        copies[4, d].start()
    for w in (2, 3, 4):
        stores[w].wait()
        for d in range(1, n_head):
            copies[w, d].wait_recv()
    for window in windows:
        window.wait()
    for one in copies.values():
        one.wait_send()


def gather(q, g, k, v, nd):
    any_spec = pl.BlockSpec(memory_space=pl.ANY)
    bf = jnp.bfloat16
    return pl.pallas_call(
        gather_kernel,
        out_shape=(
            jax.ShapeDtypeStruct((TPB, TILE, WIDTH), bf),
            jax.ShapeDtypeStruct((TPB, TILE, WIDTH), bf),
            jax.ShapeDtypeStruct((WIN, TPB, TILE, HEAD_DIM), bf),
            jax.ShapeDtypeStruct((WIN, TPB, TILE, HEAD_DIM), bf),
            jax.ShapeDtypeStruct((TPB, 2 * GROUP, TILE), jnp.float32),
        ),
        in_specs=[any_spec] * 5,
        out_specs=(any_spec,) * 5,
        scratch_shapes=[
            pltpu.VMEM((TILE, WIDTH), bf),
            pltpu.VMEM((TILE, WIDTH), bf),
            pltpu.VMEM((TILE, HEAD_DIM), bf),
            pltpu.VMEM((TILE, HEAD_DIM), bf),
            pltpu.VMEM((2 * GROUP, TILE), jnp.float32),
            pltpu.SemaphoreType.DMA((5, TPB)),
            pltpu.SemaphoreType.DMA((5, TPB)),
            pltpu.SemaphoreType.DMA((2, WIN)),
            pltpu.SemaphoreType.DMA((2, WIN)),
            pltpu.SemaphoreType.DMA((5,)),
            pltpu.SemaphoreType.DMA((5,)),
        ],
        compiler_params=pltpu.CompilerParams(collective_id=0, has_side_effects=True),
        name="gather_heads",
    )(q, g, k, v, nd)


def attend_kernel(
    pairs, count, q_ref, g_ref, nd_ref, k_ref, v_ref,
    dq_ref, dk0_ref, dv0_ref, dkp_ref, dvp_ref, acc_q, acc_k, acc_v, k_t,
):
    row = lax.broadcasted_iota(jnp.int32, (TILE, 2 * TILE), 0)
    col = lax.broadcasted_iota(jnp.int32, (TILE, 2 * TILE), 1)
    causal = row <= jnp.where(col >= TILE, col - TILE, col)

    def pair(s, qt, kt, first):
        key, value, key_t = k_ref[s, kt], v_ref[s, kt], k_t[kt]
        key_term = value_term = None
        for hp in range(GROUP // 2):
            lo, mid, hi = 2 * hp * HEAD_DIM, (2 * hp + 1) * HEAD_DIM, (2 * hp + 2) * HEAD_DIM
            query = jnp.concatenate([q_ref[qt, :, lo:mid], q_ref[qt, :, mid:hi]], axis=0)
            grad = jnp.concatenate([g_ref[qt, :, lo:mid], g_ref[qt, :, mid:hi]], axis=0)
            norm = jnp.concatenate([nd_ref[qt, 2 * hp : 2 * hp + 1], nd_ref[qt, 2 * hp + 1 : 2 * hp + 2]], axis=1)
            delta = jnp.concatenate([nd_ref[qt, GROUP + 2 * hp : GROUP + 2 * hp + 1], nd_ref[qt, GROUP + 2 * hp + 1 : GROUP + 2 * hp + 2]], axis=1)
            over = (((1,), (1,)), ((), ()))
            scores = lax.dot_general(key, query, over, preferred_element_type=jnp.float32)
            probs = jnp.exp2(scores * (SCALE * LOG2E) - norm)
            if first:
                probs = jnp.where(causal, probs, 0.0)
            prob_grad = lax.dot_general(value, grad, over, preferred_element_type=jnp.float32)
            score_grad = (SCALE * probs * (prob_grad - delta)).astype(jnp.bfloat16)
            low = probs.astype(jnp.bfloat16)
            kterm = jnp.dot(score_grad, query, preferred_element_type=jnp.float32)
            vterm = jnp.dot(low, grad, preferred_element_type=jnp.float32)
            key_term = kterm if key_term is None else key_term + kterm
            value_term = vterm if value_term is None else value_term + vterm
            qterm = jnp.dot(key_t, score_grad, preferred_element_type=jnp.float32)
            if first:
                acc_q[qt, :, lo:hi] = qterm
            else:
                acc_q[qt, :, lo:hi] += qterm
        if first:
            acc_k[kt] = key_term
            acc_v[kt] = value_term
        else:
            acc_k[kt] += key_term
            acc_v[kt] += value_term

    for s in range(WIN):
        @pl.loop(0, TPB)
        def _(t, s=s):
            k_t[t] = k_ref[s, t].T

        if s == 0:
            @pl.loop(0, TPB)
            def _(t):
                pair(0, t, t, True)
        else:
            acc_k[...] = jnp.zeros_like(acc_k)
            acc_v[...] = jnp.zeros_like(acc_v)

        @pl.loop(TPB if s == 0 else 0, count[s])
        def _(slot, s=s):
            pair(s, pairs[(s * SLOTS + slot) * 2], pairs[(s * SLOTS + slot) * 2 + 1], False)

        if s == 0:
            dk0_ref[...] = acc_k[...]
            dv0_ref[...] = acc_v[...]
        else:
            dkp_ref[s - 1] = acc_k[...].astype(jnp.bfloat16)
            dvp_ref[s - 1] = acc_v[...].astype(jnp.bfloat16)

    @pl.loop(0, TPB)
    def _(t):
        for h in range(GROUP):
            at = slice(h * HEAD_DIM, (h + 1) * HEAD_DIM)
            dq_ref[t, :, at] = acc_q[t, :, at].astype(jnp.bfloat16).T


def attend(pairs, count, q, g, nd, k, v):
    bf, f32 = jnp.bfloat16, jnp.float32
    smem = pl.BlockSpec(memory_space=pltpu.SMEM)
    vmem = pl.BlockSpec(memory_space=pltpu.VMEM)
    return pl.pallas_call(
        attend_kernel,
        out_shape=(
            jax.ShapeDtypeStruct((TPB, TILE, WIDTH), bf),
            jax.ShapeDtypeStruct((TPB, TILE, HEAD_DIM), f32),
            jax.ShapeDtypeStruct((TPB, TILE, HEAD_DIM), f32),
            jax.ShapeDtypeStruct((WIN - 1, TPB, TILE, HEAD_DIM), bf),
            jax.ShapeDtypeStruct((WIN - 1, TPB, TILE, HEAD_DIM), bf),
        ),
        in_specs=[smem, smem] + [vmem] * 5,
        out_specs=(vmem,) * 5,
        scratch_shapes=[
            pltpu.VMEM((TPB, HEAD_DIM, WIDTH), f32),
            pltpu.VMEM((TPB, TILE, HEAD_DIM), f32),
            pltpu.VMEM((TPB, TILE, HEAD_DIM), f32),
            pltpu.VMEM((TPB, HEAD_DIM, TILE), bf),
        ],
        name="attend_pairs",
    )(pairs, count, q, g, nd, k, v)


def scatter_kernel(
    dq_in, dk0, dv0, dkp, dvp, dq_out, dk_out, dv_out,
    own, got_k, got_v, sum_k, sum_v, send, recv, win_send, win_recv, own_sem,
):
    ctx, head = lax.axis_index("ctx"), lax.axis_index("head")
    n_ctx, n_head = lax.axis_size("ctx"), lax.axis_size("head")
    load = pltpu.make_async_copy(dq_in.at[head], own, own_sem.at[0])
    load.start()
    greet(ctx, head)
    wide = pl.ds(pl.multiple_of(head * WIDTH, WIDTH), WIDTH)
    slim = pl.ds(pl.multiple_of(head * HEAD_DIM, HEAD_DIM), HEAD_DIM)

    windows = []
    for which, (src, got) in enumerate(((dkp, got_k), (dvp, got_v))):
        for s in range(1, WIN):
            window = pltpu.make_async_remote_copy(
                src_ref=src.at[s - 1],
                dst_ref=got.at[s - 1],
                send_sem=win_send.at[which, s],
                recv_sem=win_recv.at[which, s],
                device_id=(wrap(ctx - s, n_ctx), head),
                device_id_type=MESH,
            )
            window.start()
            windows.append(window)

    def copy(which, d):
        j = wrap(head + d, n_head)
        src = (dq_in, sum_k, sum_v)[which].at[j]
        dst = (dq_out.at[:, wide], dk_out.at[:, slim], dv_out.at[:, slim])[which]
        return pltpu.make_async_remote_copy(
            src_ref=src,
            dst_ref=dst,
            send_sem=send.at[which, d],
            recv_sem=recv.at[which, d],
            device_id=(ctx, j),
            device_id_type=MESH,
        )

    copies = {(w, d): copy(w, d) for w in range(3) for d in range(1, n_head)}
    for d in range(1, n_head):
        copies[0, d].start()
    load.wait()
    own_q = pltpu.make_async_copy(own, dq_out.at[:, wide], own_sem.at[1])
    own_q.start()
    for window in windows:
        window.wait_recv()
    for base, got, total in ((dk0, got_k, sum_k), (dv0, got_v, sum_v)):
        value = base[...]
        for s in range(WIN - 1):
            value = value + got[s].astype(jnp.float32)
        total[...] = value.astype(jnp.bfloat16)
    for d in range(1, n_head):
        copies[1, d].start()
        copies[2, d].start()
    own_k = pltpu.make_async_copy(sum_k.at[head], dk_out.at[:, slim], own_sem.at[2])
    own_v = pltpu.make_async_copy(sum_v.at[head], dv_out.at[:, slim], own_sem.at[3])
    own_k.start()
    own_v.start()
    own_q.wait()
    own_k.wait()
    own_v.wait()
    for one in copies.values():
        one.wait()
    for window in windows:
        window.wait_send()


def scatter(dq, dk0, dv0, dkp, dvp):
    any_spec = pl.BlockSpec(memory_space=pl.ANY)
    vmem = pl.BlockSpec(memory_space=pltpu.VMEM)
    bf = jnp.bfloat16
    return pl.pallas_call(
        scatter_kernel,
        out_shape=(
            jax.ShapeDtypeStruct((TILE, TPB * WIDTH), bf),
            jax.ShapeDtypeStruct((TILE, TPB * HEAD_DIM), bf),
            jax.ShapeDtypeStruct((TILE, TPB * HEAD_DIM), bf),
        ),
        in_specs=[any_spec, vmem, vmem, any_spec, any_spec],
        out_specs=(any_spec,) * 3,
        scratch_shapes=[
            pltpu.VMEM((TILE, WIDTH), bf),
            pltpu.VMEM((WIN - 1, TPB, TILE, HEAD_DIM), bf),
            pltpu.VMEM((WIN - 1, TPB, TILE, HEAD_DIM), bf),
            pltpu.VMEM((TPB, TILE, HEAD_DIM), bf),
            pltpu.VMEM((TPB, TILE, HEAD_DIM), bf),
            pltpu.SemaphoreType.DMA((3, TPB)),
            pltpu.SemaphoreType.DMA((3, TPB)),
            pltpu.SemaphoreType.DMA((2, WIN)),
            pltpu.SemaphoreType.DMA((2, WIN)),
            pltpu.SemaphoreType.DMA((4,)),
        ],
        compiler_params=pltpu.CompilerParams(collective_id=1, has_side_effects=True),
        name="scatter_grads",
    )(dq, dk0, dv0, dkp, dvp)


def per_device(queries, keys, values, out_grad, log_norm, row_delta, tile_pairs, pair_count):
    by_head = jnp.stack([log_norm * LOG2E, row_delta], axis=0)
    by_head = by_head.reshape(2, TILE, TPB, GROUP)
    by_head = jnp.transpose(by_head, (2, 0, 3, 1)).reshape(TPB, 2 * GROUP, TILE)
    q, g, k, v, nd = gather(queries, out_grad, keys, values, by_head)
    grads = attend(tile_pairs.reshape(-1), pair_count.reshape(-1), q, g, nd, k, v)
    return scatter(*grads)


def solution(mesh):
    rows = P(("ctx", "head"), None)
    return jax.shard_map(
        per_device,
        mesh=mesh,
        in_specs=(rows,) * 6 + (P("ctx", None, None, None), P("ctx", None)),
        out_specs=(rows,) * 3,
        check_vma=False,
    )
```

```python
import functools

import jax
import jax.numpy as jnp
from jax import lax
from jax.experimental import pallas as pl
from jax.experimental.pallas import tpu as pltpu
from jax.sharding import PartitionSpec as P

HEAD_DIM = 128
TILE = 128
TPB = 8
WIN = 4
SLOTS = 16
GROUP = 4
WIDTH = GROUP * HEAD_DIM
SCALE = HEAD_DIM ** (-0.5)
LOG2E = 1.4426950408889634
MESH = pl.DeviceIdType.MESH


def wrap(value, size):
    return lax.rem(value + size, size)


def greet(ctx, head):
    n_ctx, n_head = lax.axis_size("ctx"), lax.axis_size("head")
    barrier = pltpu.get_barrier_semaphore()
    for d in range(1, n_head):
        pl.semaphore_signal(
            barrier, inc=1, device_id=(ctx, wrap(head + d, n_head)), device_id_type=MESH
        )
    for s in range(1, WIN):
        for there in (wrap(ctx + s, n_ctx), wrap(ctx - s, n_ctx)):
            pl.semaphore_signal(barrier, inc=1, device_id=(there, head), device_id_type=MESH)
    pl.semaphore_wait(barrier, n_head - 1 + 2 * (WIN - 1))


def gather_kernel(
    q_in, g_in, k_in, v_in, nd_in, q_out, g_out, k_out, v_out, nd_out,
    q_tmp, g_tmp, k_tmp, v_tmp, nd_tmp, send, recv, win_send, win_recv, own_in, own_out,
):
    ctx, head = lax.axis_index("ctx"), lax.axis_index("head")
    n_ctx, n_head = lax.axis_size("ctx"), lax.axis_size("head")

    def cut(which, j):
        if which == 0:
            return k_in.at[:, pl.ds(pl.multiple_of(j * HEAD_DIM, HEAD_DIM), HEAD_DIM)]
        if which == 1:
            return v_in.at[:, pl.ds(pl.multiple_of(j * HEAD_DIM, HEAD_DIM), HEAD_DIM)]
        if which == 2:
            return nd_in.at[j]
        if which == 3:
            return q_in.at[:, pl.ds(pl.multiple_of(j * WIDTH, WIDTH), WIDTH)]
        return g_in.at[:, pl.ds(pl.multiple_of(j * WIDTH, WIDTH), WIDTH)]

    def place(which, t):
        if which == 0:
            return k_out.at[0, t]
        if which == 1:
            return v_out.at[0, t]
        return (nd_out, q_out, g_out)[which - 2].at[t]

    temps = (k_tmp, v_tmp, nd_tmp, q_tmp, g_tmp)
    loads = [
        pltpu.make_async_copy(cut(w, head), temps[w], own_in.at[w]) for w in range(5)
    ]
    for load in loads:
        load.start()

    greet(ctx, head)

    def copy(which, d):
        j = wrap(head + d, n_head)
        return pltpu.make_async_remote_copy(
            src_ref=cut(which, j),
            dst_ref=place(which, head),
            send_sem=send.at[which, d],
            recv_sem=recv.at[which, d],
            device_id=(ctx, j),
            device_id_type=MESH,
        )

    copies = {(w, d): copy(w, d) for w in range(5) for d in range(1, n_head)}
    for w in (0, 1, 2, 3):
        for d in range(1, n_head):
            copies[w, d].start()
    stores = [
        pltpu.make_async_copy(temps[w], place(w, head), own_out.at[w]) for w in range(5)
    ]
    for w in range(5):
        loads[w].wait()
        stores[w].start()
    def window(which, source, s, slot, hop):
        out = (k_out, v_out)[which]
        return pltpu.make_async_remote_copy(
            src_ref=out.at[source],
            dst_ref=out.at[s],
            send_sem=win_send.at[which, slot],
            recv_sem=win_recv.at[which, s],
            device_id=(wrap(ctx + hop, n_ctx), head),
            device_id_type=MESH,
        )

    even = lax.rem(ctx, 2) == 0
    for which in (0, 1):
        stores[which].wait()
        for d in range(1, n_head):
            copies[which, d].wait_recv()

        @pl.when(even)
        def _(which=which):
            window(which, 0, 2, 1, 2).start()
            window(which, 0, 1, 0, 1).start()

        @pl.when(jnp.logical_not(even))
        def _(which=which):
            window(which, 0, 1, 0, 1).start()
            window(which, 0, 3, 1, 3).start()

    for d in range(1, n_head):
        copies[4, d].start()

    @pl.when(even)
    def _():
        for which in (0, 1):
            window(which, 0, 1, 0, 1).wait_recv()
            window(which, 1, 2, 2, 1).start()
        for which in (0, 1):
            window(which, 0, 2, 0, 1).wait_recv()
            window(which, 2, 3, 3, 1).start()
        for which in (0, 1):
            window(which, 0, 3, 0, 1).wait_recv()
            window(which, 0, 2, 1, 2).wait_send()
            window(which, 0, 1, 0, 1).wait_send()
            window(which, 1, 2, 2, 1).wait_send()
            window(which, 2, 3, 3, 1).wait_send()

    @pl.when(jnp.logical_not(even))
    def _():
        for which in (0, 1):
            for s in range(1, WIN):
                window(which, 0, s, 0, 1).wait_recv()
            window(which, 0, 1, 0, 1).wait_send()
            window(which, 0, 3, 1, 3).wait_send()

    for w in (2, 3, 4):
        stores[w].wait()
        for d in range(1, n_head):
            copies[w, d].wait_recv()
    for one in copies.values():
        one.wait_send()


def gather(q, g, k, v, nd):
    any_spec = pl.BlockSpec(memory_space=pl.ANY)
    bf = jnp.bfloat16
    return pl.pallas_call(
        gather_kernel,
        out_shape=(
            jax.ShapeDtypeStruct((TPB, TILE, WIDTH), bf),
            jax.ShapeDtypeStruct((TPB, TILE, WIDTH), bf),
            jax.ShapeDtypeStruct((WIN, TPB, TILE, HEAD_DIM), bf),
            jax.ShapeDtypeStruct((WIN, TPB, TILE, HEAD_DIM), bf),
            jax.ShapeDtypeStruct((TPB, 2 * GROUP, TILE), jnp.float32),
        ),
        in_specs=[any_spec] * 5,
        out_specs=(any_spec,) * 5,
        scratch_shapes=[
            pltpu.VMEM((TILE, WIDTH), bf),
            pltpu.VMEM((TILE, WIDTH), bf),
            pltpu.VMEM((TILE, HEAD_DIM), bf),
            pltpu.VMEM((TILE, HEAD_DIM), bf),
            pltpu.VMEM((2 * GROUP, TILE), jnp.float32),
            pltpu.SemaphoreType.DMA((5, TPB)),
            pltpu.SemaphoreType.DMA((5, TPB)),
            pltpu.SemaphoreType.DMA((2, WIN)),
            pltpu.SemaphoreType.DMA((2, WIN)),
            pltpu.SemaphoreType.DMA((5,)),
            pltpu.SemaphoreType.DMA((5,)),
        ],
        compiler_params=pltpu.CompilerParams(collective_id=0, has_side_effects=True),
        name="gather_heads",
    )(q, g, k, v, nd)


def attend_kernel(
    pairs, count, q_ref, g_ref, nd_ref, k_ref, v_ref,
    dq_ref, dk0_ref, dv0_ref, dkp_ref, dvp_ref, acc_q, acc_k, acc_v, k_t,
):
    row = lax.broadcasted_iota(jnp.int32, (TILE, 2 * TILE), 0)
    col = lax.broadcasted_iota(jnp.int32, (TILE, 2 * TILE), 1)
    causal = row <= jnp.where(col >= TILE, col - TILE, col)

    def pair(s, qt, kt, first):
        key, value, key_t = k_ref[s, kt], v_ref[s, kt], k_t[kt]
        key_term = value_term = None
        for hp in range(GROUP // 2):
            lo, mid, hi = 2 * hp * HEAD_DIM, (2 * hp + 1) * HEAD_DIM, (2 * hp + 2) * HEAD_DIM
            query = jnp.concatenate([q_ref[qt, :, lo:mid], q_ref[qt, :, mid:hi]], axis=0)
            grad = jnp.concatenate([g_ref[qt, :, lo:mid], g_ref[qt, :, mid:hi]], axis=0)
            norm = jnp.concatenate([nd_ref[qt, 2 * hp : 2 * hp + 1], nd_ref[qt, 2 * hp + 1 : 2 * hp + 2]], axis=1)
            delta = jnp.concatenate([nd_ref[qt, GROUP + 2 * hp : GROUP + 2 * hp + 1], nd_ref[qt, GROUP + 2 * hp + 1 : GROUP + 2 * hp + 2]], axis=1)
            over = (((1,), (1,)), ((), ()))
            scores = lax.dot_general(key, query, over, preferred_element_type=jnp.float32)
            probs = jnp.exp2(scores * (SCALE * LOG2E) - norm)
            if first:
                probs = jnp.where(causal, probs, 0.0)
            prob_grad = lax.dot_general(value, grad, over, preferred_element_type=jnp.float32)
            score_grad = (SCALE * probs * (prob_grad - delta)).astype(jnp.bfloat16)
            low = probs.astype(jnp.bfloat16)
            kterm = jnp.dot(score_grad, query, preferred_element_type=jnp.float32)
            vterm = jnp.dot(low, grad, preferred_element_type=jnp.float32)
            key_term = kterm if key_term is None else key_term + kterm
            value_term = vterm if value_term is None else value_term + vterm
            qterm = jnp.dot(key_t, score_grad, preferred_element_type=jnp.float32)
            if first:
                acc_q[qt, :, lo:hi] = qterm
            else:
                acc_q[qt, :, lo:hi] += qterm
        if first:
            acc_k[kt] = key_term
            acc_v[kt] = value_term
        else:
            acc_k[kt] += key_term
            acc_v[kt] += value_term

    for s in range(WIN):
        @pl.loop(0, TPB)
        def _(t, s=s):
            k_t[t] = k_ref[s, t].T

        if s == 0:
            @pl.loop(0, TPB)
            def _(t):
                pair(0, t, t, True)
        else:
            acc_k[...] = jnp.zeros_like(acc_k)
            acc_v[...] = jnp.zeros_like(acc_v)

        @pl.loop(TPB if s == 0 else 0, count[s])
        def _(slot, s=s):
            pair(s, pairs[(s * SLOTS + slot) * 2], pairs[(s * SLOTS + slot) * 2 + 1], False)

        if s == 0:
            dk0_ref[...] = acc_k[...]
            dv0_ref[...] = acc_v[...]
        else:
            dkp_ref[s - 1] = acc_k[...].astype(jnp.bfloat16)
            dvp_ref[s - 1] = acc_v[...].astype(jnp.bfloat16)

    @pl.loop(0, TPB)
    def _(t):
        for h in range(GROUP):
            at = slice(h * HEAD_DIM, (h + 1) * HEAD_DIM)
            dq_ref[t, :, at] = acc_q[t, :, at].astype(jnp.bfloat16).T


def attend(pairs, count, q, g, nd, k, v):
    bf, f32 = jnp.bfloat16, jnp.float32
    smem = pl.BlockSpec(memory_space=pltpu.SMEM)
    vmem = pl.BlockSpec(memory_space=pltpu.VMEM)
    return pl.pallas_call(
        attend_kernel,
        out_shape=(
            jax.ShapeDtypeStruct((TPB, TILE, WIDTH), bf),
            jax.ShapeDtypeStruct((TPB, TILE, HEAD_DIM), f32),
            jax.ShapeDtypeStruct((TPB, TILE, HEAD_DIM), f32),
            jax.ShapeDtypeStruct((WIN - 1, TPB, TILE, HEAD_DIM), bf),
            jax.ShapeDtypeStruct((WIN - 1, TPB, TILE, HEAD_DIM), bf),
        ),
        in_specs=[smem, smem] + [vmem] * 5,
        out_specs=(vmem,) * 5,
        scratch_shapes=[
            pltpu.VMEM((TPB, HEAD_DIM, WIDTH), f32),
            pltpu.VMEM((TPB, TILE, HEAD_DIM), f32),
            pltpu.VMEM((TPB, TILE, HEAD_DIM), f32),
            pltpu.VMEM((TPB, HEAD_DIM, TILE), bf),
        ],
        name="attend_pairs",
    )(pairs, count, q, g, nd, k, v)


def scatter_kernel(
    dq_in, dk0, dv0, dkp, dvp, dq_out, dk_out, dv_out,
    own, got_k, got_v, add_k, add_v, tmp_k, tmp_v, sum_k, sum_v, send, recv, win_send, win_recv, own_sem,
):
    ctx, head = lax.axis_index("ctx"), lax.axis_index("head")
    n_ctx, n_head = lax.axis_size("ctx"), lax.axis_size("head")
    load = pltpu.make_async_copy(dq_in.at[head], own, own_sem.at[0])
    load.start()
    greet(ctx, head)
    wide = pl.ds(pl.multiple_of(head * WIDTH, WIDTH), WIDTH)
    slim = pl.ds(pl.multiple_of(head * HEAD_DIM, HEAD_DIM), HEAD_DIM)

    even = lax.rem(ctx, 2) == 0
    parts, gots = (dkp, dvp), (got_k, got_v)
    adds, tmps = (add_k, add_v), (tmp_k, tmp_v)

    def part(which, src, slot, sem, back):
        return pltpu.make_async_remote_copy(
            src_ref=src,
            dst_ref=gots[which].at[slot],
            send_sem=win_send.at[which, sem],
            recv_sem=win_recv.at[which, slot],
            device_id=(wrap(ctx - back, n_ctx), head),
            device_id_type=MESH,
        )

    def odd_parts(which):
        return [part(which, parts[which].at[s], s, s, 1) for s in (1, 2, 0)]

    def even_parts(which):
        return [
            part(which, adds[which].at[0], 3, 0, 1),
            part(which, adds[which].at[1], 4, 1, 2),
            part(which, parts[which].at[2], 4, 2, 3),
        ]

    @pl.when(jnp.logical_not(even))
    def _():
        for i in range(WIN - 1):
            for which in (0, 1):
                odd_parts(which)[i].start()

    @pl.when(even)
    def _():
        for which in (0, 1):
            even_parts(which)[2].start()

    def copy(which, d):
        j = wrap(head + d, n_head)
        src = (dq_in, sum_k, sum_v)[which].at[j]
        dst = (dq_out.at[:, wide], dk_out.at[:, slim], dv_out.at[:, slim])[which]
        return pltpu.make_async_remote_copy(
            src_ref=src,
            dst_ref=dst,
            send_sem=send.at[which, d],
            recv_sem=recv.at[which, d],
            device_id=(ctx, j),
            device_id_type=MESH,
        )

    copies = {(w, d): copy(w, d) for w in range(3) for d in range(1, n_head)}
    for d in range(1, n_head):
        copies[0, d].start()
    load.wait()
    own_q = pltpu.make_async_copy(own, dq_out.at[:, wide], own_sem.at[1])
    own_q.start()
    loads = [
        pltpu.make_async_copy(parts[which].at[i], tmps[which].at[i], own_sem.at[4 + 2 * which + i])
        for i in (0, 1)
        for which in (0, 1)
    ]

    @pl.when(even)
    def _():
        for one in loads:
            one.start()
        for one in loads:
            one.wait()
        for i in (0, 1):
            for which in (0, 1):
                part(which, parts[which].at[0], i + 1, 0, 1).wait_recv()
                mine = tmps[which][i].astype(jnp.float32)
                theirs = gots[which][i + 1].astype(jnp.float32)
                adds[which][i] = (mine + theirs).astype(jnp.bfloat16)
                even_parts(which)[i].start()
        for which in (0, 1):
            part(which, parts[which].at[0], 0, 0, 1).wait_recv()
            part(which, parts[which].at[0], 4, 0, 1).wait_recv()
            value = (dk0, dv0)[which][...]
            value = value + gots[which][0].astype(jnp.float32)
            value = value + gots[which][4].astype(jnp.float32)
            (sum_k, sum_v)[which][...] = value.astype(jnp.bfloat16)

    @pl.when(jnp.logical_not(even))
    def _():
        for which in (0, 1):
            part(which, parts[which].at[0], 3, 0, 1).wait_recv()
            part(which, parts[which].at[0], 4, 0, 1).wait_recv()
            value = (dk0, dv0)[which][...]
            value = value + gots[which][3].astype(jnp.float32)
            value = value + gots[which][4].astype(jnp.float32)
            (sum_k, sum_v)[which][...] = value.astype(jnp.bfloat16)

    for d in range(1, n_head):
        copies[1, d].start()
        copies[2, d].start()
    own_k = pltpu.make_async_copy(sum_k.at[head], dk_out.at[:, slim], own_sem.at[2])
    own_v = pltpu.make_async_copy(sum_v.at[head], dv_out.at[:, slim], own_sem.at[3])
    own_k.start()
    own_v.start()
    own_q.wait()
    own_k.wait()
    own_v.wait()
    for one in copies.values():
        one.wait()

    @pl.when(even)
    def _():
        for which in (0, 1):
            for one in even_parts(which):
                one.wait_send()

    @pl.when(jnp.logical_not(even))
    def _():
        for which in (0, 1):
            for one in odd_parts(which):
                one.wait_send()


def scatter(dq, dk0, dv0, dkp, dvp):
    any_spec = pl.BlockSpec(memory_space=pl.ANY)
    vmem = pl.BlockSpec(memory_space=pltpu.VMEM)
    bf = jnp.bfloat16
    return pl.pallas_call(
        scatter_kernel,
        out_shape=(
            jax.ShapeDtypeStruct((TILE, TPB * WIDTH), bf),
            jax.ShapeDtypeStruct((TILE, TPB * HEAD_DIM), bf),
            jax.ShapeDtypeStruct((TILE, TPB * HEAD_DIM), bf),
        ),
        in_specs=[any_spec, vmem, vmem, any_spec, any_spec],
        out_specs=(any_spec,) * 3,
        scratch_shapes=[
            pltpu.VMEM((TILE, WIDTH), bf),
            pltpu.VMEM((5, TPB, TILE, HEAD_DIM), bf),
            pltpu.VMEM((5, TPB, TILE, HEAD_DIM), bf),
            pltpu.VMEM((2, TPB, TILE, HEAD_DIM), bf),
            pltpu.VMEM((2, TPB, TILE, HEAD_DIM), bf),
            pltpu.VMEM((2, TPB, TILE, HEAD_DIM), bf),
            pltpu.VMEM((2, TPB, TILE, HEAD_DIM), bf),
            pltpu.VMEM((TPB, TILE, HEAD_DIM), bf),
            pltpu.VMEM((TPB, TILE, HEAD_DIM), bf),
            pltpu.SemaphoreType.DMA((3, TPB)),
            pltpu.SemaphoreType.DMA((3, TPB)),
            pltpu.SemaphoreType.DMA((2, WIN)),
            pltpu.SemaphoreType.DMA((2, 5)),
            pltpu.SemaphoreType.DMA((8,)),
        ],
        compiler_params=pltpu.CompilerParams(collective_id=1, has_side_effects=True),
        name="scatter_grads",
    )(dq, dk0, dv0, dkp, dvp)


def per_device(queries, keys, values, out_grad, log_norm, row_delta, tile_pairs, pair_count):
    by_head = jnp.stack([log_norm * LOG2E, row_delta], axis=0)
    by_head = by_head.reshape(2, TILE, TPB, GROUP)
    by_head = jnp.transpose(by_head, (2, 0, 3, 1)).reshape(TPB, 2 * GROUP, TILE)
    q, g, k, v, nd = gather(queries, out_grad, keys, values, by_head)
    grads = attend(tile_pairs.reshape(-1), pair_count.reshape(-1), q, g, nd, k, v)
    return scatter(*grads)


def solution(mesh):
    rows = P(("ctx", "head"), None)
    return jax.shard_map(
        per_device,
        mesh=mesh,
        in_specs=(rows,) * 6 + (P("ctx", None, None, None), P("ctx", None)),
        out_specs=(rows,) * 3,
        check_vma=False,
    )
```

```python
import functools

import jax
import jax.numpy as jnp
from jax import lax
from jax.experimental import pallas as pl
from jax.experimental.pallas import tpu as pltpu
from jax.sharding import PartitionSpec as P

HEAD_DIM = 128
TILE = 128
TPB = 8
WIN = 4
SLOTS = 16
PAIRS = 2
DIAGONALS = 2
GROUP = 4
WIDTH = GROUP * HEAD_DIM
SCALE = HEAD_DIM ** (-0.5)
LOG2E = 1.4426950408889634
MESH = pl.DeviceIdType.MESH


def wrap(value, size):
    return lax.rem(value + size, size)


def greet(ctx, head):
    n_ctx, n_head = lax.axis_size("ctx"), lax.axis_size("head")
    barrier = pltpu.get_barrier_semaphore()
    for d in range(1, n_head):
        pl.semaphore_signal(
            barrier, inc=1, device_id=(ctx, wrap(head + d, n_head)), device_id_type=MESH
        )
    for s in range(1, WIN):
        for there in (wrap(ctx + s, n_ctx), wrap(ctx - s, n_ctx)):
            pl.semaphore_signal(barrier, inc=1, device_id=(there, head), device_id_type=MESH)
    pl.semaphore_wait(barrier, n_head - 1 + 2 * (WIN - 1))


def gather_kernel(
    q_in, g_in, k_in, v_in, nd_in, q_out, g_out, k_out, v_out, nd_out,
    q_tmp, g_tmp, k_tmp, v_tmp, nd_tmp, send, recv, win_send, win_recv, own_in, own_out,
):
    ctx, head = lax.axis_index("ctx"), lax.axis_index("head")
    n_ctx, n_head = lax.axis_size("ctx"), lax.axis_size("head")

    def cut(which, j):
        if which == 0:
            return k_in.at[:, pl.ds(pl.multiple_of(j * HEAD_DIM, HEAD_DIM), HEAD_DIM)]
        if which == 1:
            return v_in.at[:, pl.ds(pl.multiple_of(j * HEAD_DIM, HEAD_DIM), HEAD_DIM)]
        if which == 2:
            return nd_in.at[j]
        if which == 3:
            return q_in.at[:, pl.ds(pl.multiple_of(j * WIDTH, WIDTH), WIDTH)]
        return g_in.at[:, pl.ds(pl.multiple_of(j * WIDTH, WIDTH), WIDTH)]

    def place(which, t):
        if which == 0:
            return k_out.at[0, t]
        if which == 1:
            return v_out.at[0, t]
        return (nd_out, q_out, g_out)[which - 2].at[t]

    temps = (k_tmp, v_tmp, nd_tmp, q_tmp, g_tmp)
    loads = [
        pltpu.make_async_copy(cut(w, head), temps[w], own_in.at[w]) for w in range(5)
    ]
    for load in loads:
        load.start()

    greet(ctx, head)

    def copy(which, d):
        j = wrap(head + d, n_head)
        return pltpu.make_async_remote_copy(
            src_ref=cut(which, j),
            dst_ref=place(which, head),
            send_sem=send.at[which, d],
            recv_sem=recv.at[which, d],
            device_id=(ctx, j),
            device_id_type=MESH,
        )

    copies = {(w, d): copy(w, d) for w in range(5) for d in range(1, n_head)}
    for w in (0, 1, 2, 3):
        for d in range(1, n_head):
            copies[w, d].start()
    stores = [
        pltpu.make_async_copy(temps[w], place(w, head), own_out.at[w]) for w in range(5)
    ]
    for w in range(5):
        loads[w].wait()
        stores[w].start()
    def window(which, source, s, slot, hop):
        out = (k_out, v_out)[which]
        return pltpu.make_async_remote_copy(
            src_ref=out.at[source],
            dst_ref=out.at[s],
            send_sem=win_send.at[which, slot],
            recv_sem=win_recv.at[which, s],
            device_id=(wrap(ctx + hop, n_ctx), head),
            device_id_type=MESH,
        )

    even = lax.rem(ctx, 2) == 0
    for which in (0, 1):
        stores[which].wait()
        for d in range(1, n_head):
            copies[which, d].wait_recv()

        @pl.when(even)
        def _(which=which):
            window(which, 0, 2, 1, 2).start()
            window(which, 0, 1, 0, 1).start()

        @pl.when(jnp.logical_not(even))
        def _(which=which):
            window(which, 0, 1, 0, 1).start()
            window(which, 0, 3, 1, 3).start()

    for d in range(1, n_head):
        copies[4, d].start()

    @pl.when(even)
    def _():
        for which in (0, 1):
            window(which, 0, 1, 0, 1).wait_recv()
            window(which, 1, 2, 2, 1).start()
        for which in (0, 1):
            window(which, 0, 2, 0, 1).wait_recv()
            window(which, 2, 3, 3, 1).start()
        for which in (0, 1):
            window(which, 0, 3, 0, 1).wait_recv()
            window(which, 0, 2, 1, 2).wait_send()
            window(which, 0, 1, 0, 1).wait_send()
            window(which, 1, 2, 2, 1).wait_send()
            window(which, 2, 3, 3, 1).wait_send()

    @pl.when(jnp.logical_not(even))
    def _():
        for which in (0, 1):
            for s in range(1, WIN):
                window(which, 0, s, 0, 1).wait_recv()
            window(which, 0, 1, 0, 1).wait_send()
            window(which, 0, 3, 1, 3).wait_send()

    for w in (2, 3, 4):
        stores[w].wait()
        for d in range(1, n_head):
            copies[w, d].wait_recv()
    for one in copies.values():
        one.wait_send()


def gather(q, g, k, v, nd):
    any_spec = pl.BlockSpec(memory_space=pl.ANY)
    bf = jnp.bfloat16
    return pl.pallas_call(
        gather_kernel,
        out_shape=(
            jax.ShapeDtypeStruct((TPB, TILE, WIDTH), bf),
            jax.ShapeDtypeStruct((TPB, TILE, WIDTH), bf),
            jax.ShapeDtypeStruct((WIN, TPB, TILE, HEAD_DIM), bf),
            jax.ShapeDtypeStruct((WIN, TPB, TILE, HEAD_DIM), bf),
            jax.ShapeDtypeStruct((TPB, 2 * GROUP, TILE), jnp.float32),
        ),
        in_specs=[any_spec] * 5,
        out_specs=(any_spec,) * 5,
        scratch_shapes=[
            pltpu.VMEM((TILE, WIDTH), bf),
            pltpu.VMEM((TILE, WIDTH), bf),
            pltpu.VMEM((TILE, HEAD_DIM), bf),
            pltpu.VMEM((TILE, HEAD_DIM), bf),
            pltpu.VMEM((2 * GROUP, TILE), jnp.float32),
            pltpu.SemaphoreType.DMA((5, TPB)),
            pltpu.SemaphoreType.DMA((5, TPB)),
            pltpu.SemaphoreType.DMA((2, WIN)),
            pltpu.SemaphoreType.DMA((2, WIN)),
            pltpu.SemaphoreType.DMA((5,)),
            pltpu.SemaphoreType.DMA((5,)),
        ],
        compiler_params=pltpu.CompilerParams(collective_id=0, has_side_effects=True),
        name="gather_heads",
    )(q, g, k, v, nd)


def attend_kernel(
    pairs, count, q_ref, g_ref, nd_ref, k_ref, v_ref,
    dq_ref, dk0_ref, dv0_ref, dkp_ref, dvp_ref, acc_q, acc_k, acc_v, k_t, q_list, k_list,
):
    row = lax.broadcasted_iota(jnp.int32, (TILE, 2 * TILE), 0)
    col = lax.broadcasted_iota(jnp.int32, (TILE, 2 * TILE), 1)
    causal = row <= jnp.where(col >= TILE, col - TILE, col)
    tiles = WIN * TPB
    over = (((1,), (1,)), ((), ()))

    def heads(ref, qt, first, n):
        return jnp.concatenate(
            [ref[qt, :, h * HEAD_DIM : (h + 1) * HEAD_DIM] for h in range(first, first + n)],
            axis=0,
        )

    def row_of(qt, at):
        return jnp.concatenate([nd_ref[qt, at : at + 1], nd_ref[qt, at + 1 : at + 2]], axis=1)

    def terms(qt, kt, diagonal):
        key, value = k_ref[kt], v_ref[kt]
        grads, lows = [], []
        for at in range(0, GROUP, 2):
            scores = lax.dot_general(
                key, heads(q_ref, qt, at, 2), over, preferred_element_type=jnp.float32
            )
            prob_grad = lax.dot_general(
                value, heads(g_ref, qt, at, 2), over, preferred_element_type=jnp.float32
            )
            probs = jnp.exp2(scores * (SCALE * LOG2E) - row_of(qt, at))
            if diagonal:
                probs = jnp.where(causal, probs, 0.0)
            score_grad = SCALE * probs * (prob_grad - row_of(qt, GROUP + at))
            grads.append(score_grad.astype(jnp.bfloat16))
            lows.append(probs.astype(jnp.bfloat16))
        score_grad = jnp.concatenate(grads, axis=1)
        low = jnp.concatenate(lows, axis=1)
        return (
            jnp.dot(k_t[kt], score_grad, preferred_element_type=jnp.float32),
            jnp.dot(score_grad, heads(q_ref, qt, 0, GROUP), preferred_element_type=jnp.float32),
            jnp.dot(low, heads(g_ref, qt, 0, GROUP), preferred_element_type=jnp.float32),
        )

    @pl.loop(0, tiles // 4)
    def _(t):
        for i in range(4):
            k_t[4 * t + i] = k_ref[4 * t + i].T

    acc_k[pl.ds(TPB, tiles - TPB + 1)] = jnp.zeros((tiles - TPB + 1, TILE, HEAD_DIM), jnp.float32)
    acc_v[pl.ds(TPB, tiles - TPB + 1)] = jnp.zeros((tiles - TPB + 1, TILE, HEAD_DIM), jnp.float32)
    acc_q[TPB] = jnp.zeros((HEAD_DIM, WIDTH), jnp.float32)

    def fill(s, total):
        first = TPB if s == 0 else 0

        def put(slot, at):
            q_list[at] = pairs[(s * SLOTS + slot) * 2]
            k_list[at] = pairs[(s * SLOTS + slot) * 2 + 1] + s * TPB
            return at + 1

        return lax.fori_loop(first, count[s], put, total)

    total = jnp.int32(0)
    for s in range(WIN):
        total = fill(s, total)
    for i in range(PAIRS - 1):
        q_list[total + i] = TPB
        k_list[total + i] = tiles

    @pl.loop(0, TPB // DIAGONALS)
    def _(step):
        found = [terms(DIAGONALS * step + i, DIAGONALS * step + i, True) for i in range(DIAGONALS)]
        for i, (query_term, key_term, value_term) in enumerate(found):
            acc_q[DIAGONALS * step + i] = query_term
            acc_k[DIAGONALS * step + i] = key_term
            acc_v[DIAGONALS * step + i] = value_term

    @pl.loop(0, lax.div(total + PAIRS - 1, PAIRS))
    def _(step):
        places = [(q_list[PAIRS * step + i], k_list[PAIRS * step + i]) for i in range(PAIRS)]
        found = [terms(lax.rem(q, TPB), lax.rem(k, tiles), False) for q, k in places]
        for (q, k), (query_term, key_term, value_term) in zip(places, found):
            acc_q[q] += query_term
            acc_k[k] += key_term
            acc_v[k] += value_term

    dk0_ref[...] = acc_k[pl.ds(0, TPB)]
    dv0_ref[...] = acc_v[pl.ds(0, TPB)]
    dkp_ref[...] = acc_k[pl.ds(TPB, tiles - TPB)].astype(jnp.bfloat16)
    dvp_ref[...] = acc_v[pl.ds(TPB, tiles - TPB)].astype(jnp.bfloat16)

    @pl.loop(0, TPB)
    def _(t):
        for h in range(GROUP):
            at = slice(h * HEAD_DIM, (h + 1) * HEAD_DIM)
            dq_ref[t, :, at] = acc_q[t, :, at].astype(jnp.bfloat16).T


def attend(pairs, count, q, g, nd, k, v):
    bf, f32 = jnp.bfloat16, jnp.float32
    smem = pl.BlockSpec(memory_space=pltpu.SMEM)
    vmem = pl.BlockSpec(memory_space=pltpu.VMEM)
    return pl.pallas_call(
        attend_kernel,
        out_shape=(
            jax.ShapeDtypeStruct((TPB, TILE, WIDTH), bf),
            jax.ShapeDtypeStruct((TPB, TILE, HEAD_DIM), f32),
            jax.ShapeDtypeStruct((TPB, TILE, HEAD_DIM), f32),
            jax.ShapeDtypeStruct(((WIN - 1) * TPB, TILE, HEAD_DIM), bf),
            jax.ShapeDtypeStruct(((WIN - 1) * TPB, TILE, HEAD_DIM), bf),
        ),
        in_specs=[smem, smem] + [vmem] * 5,
        out_specs=(vmem,) * 5,
        scratch_shapes=[
            pltpu.VMEM((TPB + 1, HEAD_DIM, WIDTH), f32),
            pltpu.VMEM((WIN * TPB + 1, TILE, HEAD_DIM), f32),
            pltpu.VMEM((WIN * TPB + 1, TILE, HEAD_DIM), f32),
            pltpu.VMEM((WIN * TPB, HEAD_DIM, TILE), bf),
            pltpu.SMEM((WIN * SLOTS + PAIRS,), jnp.int32),
            pltpu.SMEM((WIN * SLOTS + PAIRS,), jnp.int32),
        ],
        name="attend_pairs",
    )(pairs, count, q, g, nd, k, v)


def scatter_kernel(
    dq_in, dk0, dv0, dkp, dvp, dq_out, dk_out, dv_out,
    own, got_k, got_v, add_k, add_v, tmp_k, tmp_v, sum_k, sum_v, send, recv, win_send, win_recv, own_sem,
):
    ctx, head = lax.axis_index("ctx"), lax.axis_index("head")
    n_ctx, n_head = lax.axis_size("ctx"), lax.axis_size("head")
    load = pltpu.make_async_copy(dq_in.at[head], own, own_sem.at[0])
    load.start()
    greet(ctx, head)
    wide = pl.ds(pl.multiple_of(head * WIDTH, WIDTH), WIDTH)
    slim = pl.ds(pl.multiple_of(head * HEAD_DIM, HEAD_DIM), HEAD_DIM)

    even = lax.rem(ctx, 2) == 0
    parts, gots = (dkp, dvp), (got_k, got_v)
    adds, tmps = (add_k, add_v), (tmp_k, tmp_v)

    def part(which, src, slot, sem, back):
        return pltpu.make_async_remote_copy(
            src_ref=src,
            dst_ref=gots[which].at[slot],
            send_sem=win_send.at[which, sem],
            recv_sem=win_recv.at[which, slot],
            device_id=(wrap(ctx - back, n_ctx), head),
            device_id_type=MESH,
        )

    def odd_parts(which):
        return [part(which, parts[which].at[s], s, s, 1) for s in (1, 2, 0)]

    def even_parts(which):
        return [
            part(which, adds[which].at[0], 3, 0, 1),
            part(which, adds[which].at[1], 4, 1, 2),
            part(which, parts[which].at[2], 4, 2, 3),
        ]

    @pl.when(jnp.logical_not(even))
    def _():
        for i in range(WIN - 1):
            for which in (0, 1):
                odd_parts(which)[i].start()

    @pl.when(even)
    def _():
        for which in (0, 1):
            even_parts(which)[2].start()

    def copy(which, d):
        j = wrap(head + d, n_head)
        src = (dq_in, sum_k, sum_v)[which].at[j]
        dst = (dq_out.at[:, wide], dk_out.at[:, slim], dv_out.at[:, slim])[which]
        return pltpu.make_async_remote_copy(
            src_ref=src,
            dst_ref=dst,
            send_sem=send.at[which, d],
            recv_sem=recv.at[which, d],
            device_id=(ctx, j),
            device_id_type=MESH,
        )

    copies = {(w, d): copy(w, d) for w in range(3) for d in range(1, n_head)}
    for d in range(1, n_head):
        copies[0, d].start()
    load.wait()
    own_q = pltpu.make_async_copy(own, dq_out.at[:, wide], own_sem.at[1])
    own_q.start()
    loads = [
        pltpu.make_async_copy(parts[which].at[i], tmps[which].at[i], own_sem.at[4 + 2 * which + i])
        for i in (0, 1)
        for which in (0, 1)
    ]

    @pl.when(even)
    def _():
        for one in loads:
            one.start()
        for one in loads:
            one.wait()
        for i in (0, 1):
            for which in (0, 1):
                part(which, parts[which].at[0], i + 1, 0, 1).wait_recv()
                mine = tmps[which][i].astype(jnp.float32)
                theirs = gots[which][i + 1].astype(jnp.float32)
                adds[which][i] = (mine + theirs).astype(jnp.bfloat16)
                even_parts(which)[i].start()
        for which in (0, 1):
            part(which, parts[which].at[0], 0, 0, 1).wait_recv()
            part(which, parts[which].at[0], 4, 0, 1).wait_recv()
            value = (dk0, dv0)[which][...]
            value = value + gots[which][0].astype(jnp.float32)
            value = value + gots[which][4].astype(jnp.float32)
            (sum_k, sum_v)[which][...] = value.astype(jnp.bfloat16)

    @pl.when(jnp.logical_not(even))
    def _():
        for which in (0, 1):
            part(which, parts[which].at[0], 3, 0, 1).wait_recv()
            part(which, parts[which].at[0], 4, 0, 1).wait_recv()
            value = (dk0, dv0)[which][...]
            value = value + gots[which][3].astype(jnp.float32)
            value = value + gots[which][4].astype(jnp.float32)
            (sum_k, sum_v)[which][...] = value.astype(jnp.bfloat16)

    for d in range(1, n_head):
        copies[1, d].start()
        copies[2, d].start()
    own_k = pltpu.make_async_copy(sum_k.at[head], dk_out.at[:, slim], own_sem.at[2])
    own_v = pltpu.make_async_copy(sum_v.at[head], dv_out.at[:, slim], own_sem.at[3])
    own_k.start()
    own_v.start()
    own_q.wait()
    own_k.wait()
    own_v.wait()
    for one in copies.values():
        one.wait()

    @pl.when(even)
    def _():
        for which in (0, 1):
            for one in even_parts(which):
                one.wait_send()

    @pl.when(jnp.logical_not(even))
    def _():
        for which in (0, 1):
            for one in odd_parts(which):
                one.wait_send()


def scatter(dq, dk0, dv0, dkp, dvp):
    any_spec = pl.BlockSpec(memory_space=pl.ANY)
    vmem = pl.BlockSpec(memory_space=pltpu.VMEM)
    bf = jnp.bfloat16
    return pl.pallas_call(
        scatter_kernel,
        out_shape=(
            jax.ShapeDtypeStruct((TILE, TPB * WIDTH), bf),
            jax.ShapeDtypeStruct((TILE, TPB * HEAD_DIM), bf),
            jax.ShapeDtypeStruct((TILE, TPB * HEAD_DIM), bf),
        ),
        in_specs=[any_spec, vmem, vmem, any_spec, any_spec],
        out_specs=(any_spec,) * 3,
        scratch_shapes=[
            pltpu.VMEM((TILE, WIDTH), bf),
            pltpu.VMEM((5, TPB, TILE, HEAD_DIM), bf),
            pltpu.VMEM((5, TPB, TILE, HEAD_DIM), bf),
            pltpu.VMEM((2, TPB, TILE, HEAD_DIM), bf),
            pltpu.VMEM((2, TPB, TILE, HEAD_DIM), bf),
            pltpu.VMEM((2, TPB, TILE, HEAD_DIM), bf),
            pltpu.VMEM((2, TPB, TILE, HEAD_DIM), bf),
            pltpu.VMEM((TPB, TILE, HEAD_DIM), bf),
            pltpu.VMEM((TPB, TILE, HEAD_DIM), bf),
            pltpu.SemaphoreType.DMA((3, TPB)),
            pltpu.SemaphoreType.DMA((3, TPB)),
            pltpu.SemaphoreType.DMA((2, WIN)),
            pltpu.SemaphoreType.DMA((2, 5)),
            pltpu.SemaphoreType.DMA((8,)),
        ],
        compiler_params=pltpu.CompilerParams(collective_id=1, has_side_effects=True),
        name="scatter_grads",
    )(dq, dk0, dv0, dkp, dvp)


def per_device(queries, keys, values, out_grad, log_norm, row_delta, tile_pairs, pair_count):
    by_head = jnp.stack([log_norm * LOG2E, row_delta], axis=0)
    by_head = by_head.reshape(2, TILE, TPB, GROUP)
    by_head = jnp.transpose(by_head, (2, 0, 3, 1)).reshape(TPB, 2 * GROUP, TILE)
    q, g, k, v, nd = gather(queries, out_grad, keys, values, by_head)
    tiles = (WIN * TPB, TILE, HEAD_DIM)
    dq, dk0, dv0, dkp, dvp = attend(
        tile_pairs.reshape(-1), pair_count.reshape(-1), q, g, nd, k.reshape(tiles), v.reshape(tiles)
    )
    parts = (WIN - 1, TPB, TILE, HEAD_DIM)
    return scatter(dq, dk0, dv0, dkp.reshape(parts), dvp.reshape(parts))


def solution(mesh):
    rows = P(("ctx", "head"), None)
    return jax.shard_map(
        per_device,
        mesh=mesh,
        in_specs=(rows,) * 6 + (P("ctx", None, None, None), P("ctx", None)),
        out_specs=(rows,) * 3,
        check_vma=False,
    )
```

```python
import functools

import jax
import jax.numpy as jnp
from jax import lax
from jax.experimental import pallas as pl
from jax.experimental.pallas import tpu as pltpu
from jax.sharding import PartitionSpec as P

HEAD_DIM = 128
TILE = 128
TPB = 8
WIN = 4
SLOTS = 16
PAIRS = 2
DIAGONALS = 2
GROUP = 4
WIDTH = GROUP * HEAD_DIM
SCALE = HEAD_DIM ** (-0.5)
LOG2E = 1.4426950408889634
MESH = pl.DeviceIdType.MESH


def wrap(value, size):
    return lax.rem(value + size, size)


def greet(ctx, head, fan=False):
    n_ctx, n_head = lax.axis_size("ctx"), lax.axis_size("head")
    barrier = pltpu.get_barrier_semaphore()
    for d in range(1, n_head):
        pl.semaphore_signal(
            barrier, inc=1, device_id=(ctx, wrap(head + d, n_head)), device_id_type=MESH
        )
    for s in range(1, WIN):
        for there in (wrap(ctx + s, n_ctx), wrap(ctx - s, n_ctx)):
            pl.semaphore_signal(barrier, inc=1, device_id=(there, head), device_id_type=MESH)
    extra = 0
    if fan:
        extra = n_head - 1

        @pl.when(lax.rem(ctx, 2) == 0)
        def _():
            for d in range(1, n_head):
                for back in (1, 2):
                    pl.semaphore_signal(
                        barrier,
                        inc=1,
                        device_id=(wrap(ctx - back, n_ctx), wrap(head + d, n_head)),
                        device_id_type=MESH,
                    )

    pl.semaphore_wait(barrier, n_head - 1 + 2 * (WIN - 1) + extra)


def gather_kernel(
    q_in, g_in, k_in, v_in, nd_in, q_out, g_out, k_out, v_out, nd_out,
    q_tmp, g_tmp, k_tmp, v_tmp, nd_tmp, send, recv, fan_send, fan_recv, win_send, win_recv, own_in, own_out,
):
    ctx, head = lax.axis_index("ctx"), lax.axis_index("head")
    n_ctx, n_head = lax.axis_size("ctx"), lax.axis_size("head")

    def cut(which, j):
        if which == 0:
            return k_in.at[:, pl.ds(pl.multiple_of(j * HEAD_DIM, HEAD_DIM), HEAD_DIM)]
        if which == 1:
            return v_in.at[:, pl.ds(pl.multiple_of(j * HEAD_DIM, HEAD_DIM), HEAD_DIM)]
        if which == 2:
            return nd_in.at[j]
        if which == 3:
            return q_in.at[:, pl.ds(pl.multiple_of(j * WIDTH, WIDTH), WIDTH)]
        return g_in.at[:, pl.ds(pl.multiple_of(j * WIDTH, WIDTH), WIDTH)]

    def place(which, t):
        if which == 0:
            return k_out.at[0, t]
        if which == 1:
            return v_out.at[0, t]
        return (nd_out, q_out, g_out)[which - 2].at[t]

    temps = (k_tmp, v_tmp, nd_tmp, q_tmp, g_tmp)
    loads = [
        pltpu.make_async_copy(cut(w, head), temps[w], own_in.at[w]) for w in range(5)
    ]
    for load in loads:
        load.start()

    greet(ctx, head, fan=True)

    def copy(which, d):
        j = wrap(head + d, n_head)
        return pltpu.make_async_remote_copy(
            src_ref=cut(which, j),
            dst_ref=place(which, head),
            send_sem=send.at[which, d],
            recv_sem=recv.at[which, d],
            device_id=(ctx, j),
            device_id_type=MESH,
        )

    copies = {(w, d): copy(w, d) for w in range(5) for d in range(1, n_head)}
    even = lax.rem(ctx, 2) == 0
    reach = 2 - lax.rem(ctx, 2)

    def fan(which, d, slot):
        j = wrap(head + d, n_head)
        return pltpu.make_async_remote_copy(
            src_ref=cut(which, j),
            dst_ref=(k_out, v_out)[which].at[slot, head],
            send_sem=fan_send.at[which, d],
            recv_sem=fan_recv.at[which, slot, d],
            device_id=(wrap(ctx + reach, n_ctx), j),
            device_id_type=MESH,
        )

    for w in (0, 1):
        for d in range(1, n_head):
            copies[w, d].start()
            fan(w, d, reach).start()
        fan(w, 0, reach).start()
    for w in (2, 3):
        for d in range(1, n_head):
            copies[w, d].start()
    stores = [
        pltpu.make_async_copy(temps[w], place(w, head), own_out.at[w]) for w in range(5)
    ]
    for w in range(5):
        loads[w].wait()
        stores[w].start()
    def window(which, source, s, slot, hop):
        out = (k_out, v_out)[which]
        return pltpu.make_async_remote_copy(
            src_ref=out.at[source],
            dst_ref=out.at[s],
            send_sem=win_send.at[which, slot],
            recv_sem=win_recv.at[which, s],
            device_id=(wrap(ctx + hop, n_ctx), head),
            device_id_type=MESH,
        )

    for which in (0, 1):
        stores[which].wait()
        for d in range(1, n_head):
            copies[which, d].wait_recv()

        @pl.when(even)
        def _(which=which):
            window(which, 0, 1, 0, 1).start()

        @pl.when(jnp.logical_not(even))
        def _(which=which):
            window(which, 0, 3, 1, 3).start()

    for d in range(1, n_head):
        copies[4, d].start()

    @pl.when(even)
    def _():
        for which in (0, 1):
            for d in range(n_head):
                fan(which, d, 1).wait_recv()
            window(which, 1, 2, 2, 1).start()
        for which in (0, 1):
            for d in range(n_head):
                fan(which, d, 2).wait_recv()
            window(which, 2, 3, 3, 1).start()
        for which in (0, 1):
            window(which, 0, 3, 0, 1).wait_recv()
            window(which, 0, 1, 0, 1).wait_send()
            window(which, 1, 2, 2, 1).wait_send()
            window(which, 2, 3, 3, 1).wait_send()

    @pl.when(jnp.logical_not(even))
    def _():
        for which in (0, 1):
            for s in range(1, WIN):
                window(which, 0, s, 0, 1).wait_recv()
            window(which, 0, 3, 1, 3).wait_send()

    for w in (2, 3, 4):
        stores[w].wait()
        for d in range(1, n_head):
            copies[w, d].wait_recv()
    for one in copies.values():
        one.wait_send()
    for w in (0, 1):
        for d in range(n_head):
            fan(w, d, reach).wait_send()


def gather(q, g, k, v, nd):
    any_spec = pl.BlockSpec(memory_space=pl.ANY)
    bf = jnp.bfloat16
    return pl.pallas_call(
        gather_kernel,
        out_shape=(
            jax.ShapeDtypeStruct((TPB, TILE, WIDTH), bf),
            jax.ShapeDtypeStruct((TPB, TILE, WIDTH), bf),
            jax.ShapeDtypeStruct((WIN, TPB, TILE, HEAD_DIM), bf),
            jax.ShapeDtypeStruct((WIN, TPB, TILE, HEAD_DIM), bf),
            jax.ShapeDtypeStruct((TPB, 2 * GROUP, TILE), jnp.float32),
        ),
        in_specs=[any_spec] * 5,
        out_specs=(any_spec,) * 5,
        scratch_shapes=[
            pltpu.VMEM((TILE, WIDTH), bf),
            pltpu.VMEM((TILE, WIDTH), bf),
            pltpu.VMEM((TILE, HEAD_DIM), bf),
            pltpu.VMEM((TILE, HEAD_DIM), bf),
            pltpu.VMEM((2 * GROUP, TILE), jnp.float32),
            pltpu.SemaphoreType.DMA((5, TPB)),
            pltpu.SemaphoreType.DMA((5, TPB)),
            pltpu.SemaphoreType.DMA((2, TPB)),
            pltpu.SemaphoreType.DMA((2, WIN, TPB)),
            pltpu.SemaphoreType.DMA((2, WIN)),
            pltpu.SemaphoreType.DMA((2, WIN)),
            pltpu.SemaphoreType.DMA((5,)),
            pltpu.SemaphoreType.DMA((5,)),
        ],
        compiler_params=pltpu.CompilerParams(collective_id=0, has_side_effects=True),
        name="gather_heads",
    )(q, g, k, v, nd)


def attend_kernel(
    pairs, count, q_ref, g_ref, nd_ref, k_ref, v_ref,
    dq_ref, dk0_ref, dv0_ref, dkp_ref, dvp_ref, acc_q, acc_k, acc_v, k_t, q_list, k_list,
):
    row = lax.broadcasted_iota(jnp.int32, (TILE, 2 * TILE), 0)
    col = lax.broadcasted_iota(jnp.int32, (TILE, 2 * TILE), 1)
    causal = row <= jnp.where(col >= TILE, col - TILE, col)
    tiles = WIN * TPB
    over = (((1,), (1,)), ((), ()))

    def heads(ref, qt, first, n):
        return jnp.concatenate(
            [ref[qt, :, h * HEAD_DIM : (h + 1) * HEAD_DIM] for h in range(first, first + n)],
            axis=0,
        )

    def row_of(qt, at):
        return jnp.concatenate([nd_ref[qt, at : at + 1], nd_ref[qt, at + 1 : at + 2]], axis=1)

    def terms(qt, kt, diagonal):
        key, value = k_ref[kt], v_ref[kt]
        grads, lows = [], []
        for at in range(0, GROUP, 2):
            scores = lax.dot_general(
                key, heads(q_ref, qt, at, 2), over, preferred_element_type=jnp.float32
            )
            prob_grad = lax.dot_general(
                value, heads(g_ref, qt, at, 2), over, preferred_element_type=jnp.float32
            )
            probs = jnp.exp2(scores * (SCALE * LOG2E) - row_of(qt, at))
            if diagonal:
                probs = jnp.where(causal, probs, 0.0)
            score_grad = SCALE * probs * (prob_grad - row_of(qt, GROUP + at))
            grads.append(score_grad.astype(jnp.bfloat16))
            lows.append(probs.astype(jnp.bfloat16))
        score_grad = jnp.concatenate(grads, axis=1)
        low = jnp.concatenate(lows, axis=1)
        return (
            jnp.dot(k_t[kt], score_grad, preferred_element_type=jnp.float32),
            jnp.dot(score_grad, heads(q_ref, qt, 0, GROUP), preferred_element_type=jnp.float32),
            jnp.dot(low, heads(g_ref, qt, 0, GROUP), preferred_element_type=jnp.float32),
        )

    @pl.loop(0, tiles // 4)
    def _(t):
        for i in range(4):
            k_t[4 * t + i] = k_ref[4 * t + i].T

    acc_k[pl.ds(TPB, tiles - TPB + 1)] = jnp.zeros((tiles - TPB + 1, TILE, HEAD_DIM), jnp.float32)
    acc_v[pl.ds(TPB, tiles - TPB + 1)] = jnp.zeros((tiles - TPB + 1, TILE, HEAD_DIM), jnp.float32)
    acc_q[TPB] = jnp.zeros((HEAD_DIM, WIDTH), jnp.float32)

    def fill(s, total):
        first = TPB if s == 0 else 0

        def put(slot, at):
            q_list[at] = pairs[(s * SLOTS + slot) * 2]
            k_list[at] = pairs[(s * SLOTS + slot) * 2 + 1] + s * TPB
            return at + 1

        return lax.fori_loop(first, count[s], put, total)

    total = jnp.int32(0)
    for s in range(WIN):
        total = fill(s, total)
    for i in range(PAIRS - 1):
        q_list[total + i] = TPB
        k_list[total + i] = tiles

    @pl.loop(0, TPB // DIAGONALS)
    def _(step):
        found = [terms(DIAGONALS * step + i, DIAGONALS * step + i, True) for i in range(DIAGONALS)]
        for i, (query_term, key_term, value_term) in enumerate(found):
            acc_q[DIAGONALS * step + i] = query_term
            acc_k[DIAGONALS * step + i] = key_term
            acc_v[DIAGONALS * step + i] = value_term

    @pl.loop(0, lax.div(total + PAIRS - 1, PAIRS))
    def _(step):
        places = [(q_list[PAIRS * step + i], k_list[PAIRS * step + i]) for i in range(PAIRS)]
        found = [terms(lax.rem(q, TPB), lax.rem(k, tiles), False) for q, k in places]
        for (q, k), (query_term, key_term, value_term) in zip(places, found):
            acc_q[q] += query_term
            acc_k[k] += key_term
            acc_v[k] += value_term

    dk0_ref[...] = acc_k[pl.ds(0, TPB)]
    dv0_ref[...] = acc_v[pl.ds(0, TPB)]
    dkp_ref[...] = acc_k[pl.ds(TPB, tiles - TPB)].astype(jnp.bfloat16)
    dvp_ref[...] = acc_v[pl.ds(TPB, tiles - TPB)].astype(jnp.bfloat16)

    @pl.loop(0, TPB)
    def _(t):
        for h in range(GROUP):
            at = slice(h * HEAD_DIM, (h + 1) * HEAD_DIM)
            dq_ref[t, :, at] = acc_q[t, :, at].astype(jnp.bfloat16).T


def attend(pairs, count, q, g, nd, k, v):
    bf, f32 = jnp.bfloat16, jnp.float32
    smem = pl.BlockSpec(memory_space=pltpu.SMEM)
    vmem = pl.BlockSpec(memory_space=pltpu.VMEM)
    return pl.pallas_call(
        attend_kernel,
        out_shape=(
            jax.ShapeDtypeStruct((TPB, TILE, WIDTH), bf),
            jax.ShapeDtypeStruct((TPB, TILE, HEAD_DIM), f32),
            jax.ShapeDtypeStruct((TPB, TILE, HEAD_DIM), f32),
            jax.ShapeDtypeStruct(((WIN - 1) * TPB, TILE, HEAD_DIM), bf),
            jax.ShapeDtypeStruct(((WIN - 1) * TPB, TILE, HEAD_DIM), bf),
        ),
        in_specs=[smem, smem] + [vmem] * 5,
        out_specs=(vmem,) * 5,
        scratch_shapes=[
            pltpu.VMEM((TPB + 1, HEAD_DIM, WIDTH), f32),
            pltpu.VMEM((WIN * TPB + 1, TILE, HEAD_DIM), f32),
            pltpu.VMEM((WIN * TPB + 1, TILE, HEAD_DIM), f32),
            pltpu.VMEM((WIN * TPB, HEAD_DIM, TILE), bf),
            pltpu.SMEM((WIN * SLOTS + PAIRS,), jnp.int32),
            pltpu.SMEM((WIN * SLOTS + PAIRS,), jnp.int32),
        ],
        name="attend_pairs",
    )(pairs, count, q, g, nd, k, v)


def scatter_kernel(
    dq_in, dk0, dv0, dkp, dvp, dq_out, dk_out, dv_out,
    own, got_k, got_v, add_k, add_v, tmp_k, tmp_v, sum_k, sum_v, send, recv, win_send, win_recv, own_sem,
):
    ctx, head = lax.axis_index("ctx"), lax.axis_index("head")
    n_ctx, n_head = lax.axis_size("ctx"), lax.axis_size("head")
    load = pltpu.make_async_copy(dq_in.at[head], own, own_sem.at[0])
    load.start()
    greet(ctx, head)
    wide = pl.ds(pl.multiple_of(head * WIDTH, WIDTH), WIDTH)
    slim = pl.ds(pl.multiple_of(head * HEAD_DIM, HEAD_DIM), HEAD_DIM)

    even = lax.rem(ctx, 2) == 0
    parts, gots = (dkp, dvp), (got_k, got_v)
    adds, tmps = (add_k, add_v), (tmp_k, tmp_v)

    def part(which, src, slot, sem, back):
        return pltpu.make_async_remote_copy(
            src_ref=src,
            dst_ref=gots[which].at[slot],
            send_sem=win_send.at[which, sem],
            recv_sem=win_recv.at[which, slot],
            device_id=(wrap(ctx - back, n_ctx), head),
            device_id_type=MESH,
        )

    def odd_parts(which):
        return [part(which, parts[which].at[s], s, s, 1) for s in (1, 2, 0)]

    def even_parts(which):
        return [
            part(which, adds[which].at[0], 3, 0, 1),
            part(which, adds[which].at[1], 4, 1, 2),
            part(which, parts[which].at[2], 4, 2, 3),
        ]

    @pl.when(jnp.logical_not(even))
    def _():
        for i in range(WIN - 1):
            for which in (0, 1):
                odd_parts(which)[i].start()

    @pl.when(even)
    def _():
        for which in (0, 1):
            even_parts(which)[2].start()

    def copy(which, d):
        j = wrap(head + d, n_head)
        src = (dq_in, sum_k, sum_v)[which].at[j]
        dst = (dq_out.at[:, wide], dk_out.at[:, slim], dv_out.at[:, slim])[which]
        return pltpu.make_async_remote_copy(
            src_ref=src,
            dst_ref=dst,
            send_sem=send.at[which, d],
            recv_sem=recv.at[which, d],
            device_id=(ctx, j),
            device_id_type=MESH,
        )

    copies = {(w, d): copy(w, d) for w in range(3) for d in range(1, n_head)}
    for d in range(1, n_head):
        copies[0, d].start()
    load.wait()
    own_q = pltpu.make_async_copy(own, dq_out.at[:, wide], own_sem.at[1])
    own_q.start()
    loads = [
        pltpu.make_async_copy(parts[which].at[i], tmps[which].at[i], own_sem.at[4 + 2 * which + i])
        for i in (0, 1)
        for which in (0, 1)
    ]

    @pl.when(even)
    def _():
        for one in loads:
            one.start()
        for one in loads:
            one.wait()
        for i in (0, 1):
            for which in (0, 1):
                part(which, parts[which].at[0], i + 1, 0, 1).wait_recv()
                mine = tmps[which][i].astype(jnp.float32)
                theirs = gots[which][i + 1].astype(jnp.float32)
                adds[which][i] = (mine + theirs).astype(jnp.bfloat16)
                even_parts(which)[i].start()
        for which in (0, 1):
            part(which, parts[which].at[0], 0, 0, 1).wait_recv()
            part(which, parts[which].at[0], 4, 0, 1).wait_recv()
            value = (dk0, dv0)[which][...]
            value = value + gots[which][0].astype(jnp.float32)
            value = value + gots[which][4].astype(jnp.float32)
            (sum_k, sum_v)[which][...] = value.astype(jnp.bfloat16)

    @pl.when(jnp.logical_not(even))
    def _():
        for which in (0, 1):
            part(which, parts[which].at[0], 3, 0, 1).wait_recv()
            part(which, parts[which].at[0], 4, 0, 1).wait_recv()
            value = (dk0, dv0)[which][...]
            value = value + gots[which][3].astype(jnp.float32)
            value = value + gots[which][4].astype(jnp.float32)
            (sum_k, sum_v)[which][...] = value.astype(jnp.bfloat16)

    for d in range(1, n_head):
        copies[1, d].start()
        copies[2, d].start()
    own_k = pltpu.make_async_copy(sum_k.at[head], dk_out.at[:, slim], own_sem.at[2])
    own_v = pltpu.make_async_copy(sum_v.at[head], dv_out.at[:, slim], own_sem.at[3])
    own_k.start()
    own_v.start()
    own_q.wait()
    own_k.wait()
    own_v.wait()
    for one in copies.values():
        one.wait()

    @pl.when(even)
    def _():
        for which in (0, 1):
            for one in even_parts(which):
                one.wait_send()

    @pl.when(jnp.logical_not(even))
    def _():
        for which in (0, 1):
            for one in odd_parts(which):
                one.wait_send()


def scatter(dq, dk0, dv0, dkp, dvp):
    any_spec = pl.BlockSpec(memory_space=pl.ANY)
    vmem = pl.BlockSpec(memory_space=pltpu.VMEM)
    bf = jnp.bfloat16
    return pl.pallas_call(
        scatter_kernel,
        out_shape=(
            jax.ShapeDtypeStruct((TILE, TPB * WIDTH), bf),
            jax.ShapeDtypeStruct((TILE, TPB * HEAD_DIM), bf),
            jax.ShapeDtypeStruct((TILE, TPB * HEAD_DIM), bf),
        ),
        in_specs=[any_spec, vmem, vmem, any_spec, any_spec],
        out_specs=(any_spec,) * 3,
        scratch_shapes=[
            pltpu.VMEM((TILE, WIDTH), bf),
            pltpu.VMEM((5, TPB, TILE, HEAD_DIM), bf),
            pltpu.VMEM((5, TPB, TILE, HEAD_DIM), bf),
            pltpu.VMEM((2, TPB, TILE, HEAD_DIM), bf),
            pltpu.VMEM((2, TPB, TILE, HEAD_DIM), bf),
            pltpu.VMEM((2, TPB, TILE, HEAD_DIM), bf),
            pltpu.VMEM((2, TPB, TILE, HEAD_DIM), bf),
            pltpu.VMEM((TPB, TILE, HEAD_DIM), bf),
            pltpu.VMEM((TPB, TILE, HEAD_DIM), bf),
            pltpu.SemaphoreType.DMA((3, TPB)),
            pltpu.SemaphoreType.DMA((3, TPB)),
            pltpu.SemaphoreType.DMA((2, WIN)),
            pltpu.SemaphoreType.DMA((2, 5)),
            pltpu.SemaphoreType.DMA((8,)),
        ],
        compiler_params=pltpu.CompilerParams(collective_id=1, has_side_effects=True),
        name="scatter_grads",
    )(dq, dk0, dv0, dkp, dvp)


def per_device(queries, keys, values, out_grad, log_norm, row_delta, tile_pairs, pair_count):
    by_head = jnp.stack([log_norm * LOG2E, row_delta], axis=0)
    by_head = by_head.reshape(2, TILE, TPB, GROUP)
    by_head = jnp.transpose(by_head, (2, 0, 3, 1)).reshape(TPB, 2 * GROUP, TILE)
    q, g, k, v, nd = gather(queries, out_grad, keys, values, by_head)
    tiles = (WIN * TPB, TILE, HEAD_DIM)
    dq, dk0, dv0, dkp, dvp = attend(
        tile_pairs.reshape(-1), pair_count.reshape(-1), q, g, nd, k.reshape(tiles), v.reshape(tiles)
    )
    parts = (WIN - 1, TPB, TILE, HEAD_DIM)
    return scatter(dq, dk0, dv0, dkp.reshape(parts), dvp.reshape(parts))


def solution(mesh):
    rows = P(("ctx", "head"), None)
    return jax.shard_map(
        per_device,
        mesh=mesh,
        in_specs=(rows,) * 6 + (P("ctx", None, None, None), P("ctx", None)),
        out_specs=(rows,) * 3,
        check_vma=False,
    )
```
